32 devices in a mesh: img: 4 (over y, core), bank: 8 (over z, x).
Axes of the slice: x: 2, y: 2, z: 4, core: 2. Of those that a mesh axis runs over, the one named last changes fastest.
Arguments:
- boxes: bfloat16 [8, 256, 768], P('img'), may hold values from -80 to 80
- prototypes: bfloat16 [65536, 768], P('bank'), may hold values from -3 to 3
- counts: int32 [4, 2], P('img'), may hold values from 1 to 256, 320 in all within a row
- keep: int32 [8, 256], P('img'), may hold values 0 or 1
Outputs:
- targets: bfloat16 [8, 256, 768], P('img', 'bank')
- top_logprob: float32 [8, 256], P('img', 'bank')
- log_norm: float32 [8, 256], P('img', 'bank')
The draws below stay inside these ranges and needn't reach their ends.
Inputs may be any that keep to these rules, and one draw needn't show every extreme that they name: The counts of each group of 2 images sum to exactly 320.
All inputs are finite; a program needn't handle non-finite values. No bound on the sum of `keep` on one device may be relied on, other than what follows from the above.
Results may differ from the reference program's by a relative error of at most 0.0025.
Values sent between devices are 32-bit elements; how exact they have to be, the bound alone decides.
No kernel may reach another device: no remote copies, remote signals or barrier semaphores. Data moves between devices by JAX's collectives and lax.ppermute only.
A program may use at most 128 MiB of HBM per device.

```python
import math
import jax
import jax.numpy as jnp
import numpy as np
from jax import lax

D = 768
VDEV = 8192
BOXES = 256
IMG_DEV = 2
GROUPS = 4
IMAGES = 8
BANK = 65536
LIVE = 320
N_BANK = 8


def proto_table(key):
    raw = jax.random.normal(jax.random.fold_in(key, 11), (BANK, D), jnp.float32)
    return 3.0 * raw / jnp.sqrt(jnp.sum(raw * raw, axis=1, keepdims=True))


def draw_prototypes(key, part):
    return proto_table(key).astype(jnp.bfloat16)


def draw_boxes(key, part):
    raw = jax.random.truncated_normal(jax.random.fold_in(key, 12), -6.0, 6.0, (IMAGES, BOXES, D), jnp.float32)
    return raw.astype(jnp.bfloat16)


def set_ends(values, key, low, high):
    longest = values.shape.index(max(values.shape))
    spots = []
    for shift in (0, 1):
        where = [jax.random.randint(jax.random.fold_in(key, axis), (), 0, length) for axis, length in enumerate(values.shape)]
        where[longest] = (where[longest] + shift) % values.shape[longest]
        spots.append(tuple(where))
    return values.at[spots[0]].set(low).at[spots[1]].set(high)


def split_up(amount, total, bound, skew):
    weights = [(1 << 20) // math.isqrt(grade ** skew) + 1 for grade in range(2, amount + 1)]
    spare, holding = total - bound - (amount - 1), [1] * (amount - 1)
    while spare > 0:
        free = [i for i in range(amount - 1) if holding[i] < bound]
        whole, remaining = sum([weights[i] for i in free]), spare
        for i in free:
            addition = min(bound - holding[i], max(1, remaining * weights[i] // whole), spare)
            holding[i] = holding[i] + addition
            spare = spare - addition
    return np.array([bound] + holding)


def ragged_sizes(own_key, amount, total, bound, skew):
    if amount == 2:
        one = jax.random.randint(own_key, (), max(1, total - bound), min(bound, total - 1) + 1)
        return jnp.stack([one, total - one])
    tallies = jnp.asarray(split_up(amount, total, bound, skew), jnp.int32)
    twos = (amount - 1) // 2
    donor, receiver = tallies[1:1 + 2 * twos:2], tallies[2:2 + 2 * twos:2]
    margin = jnp.minimum(donor - 1, bound - receiver)
    moved = jax.random.randint(jax.random.fold_in(own_key, 1), (twos,), 0, 1 << 20) % (margin + 1)
    tallies = tallies.at[1:1 + 2 * twos:2].set(donor - moved).at[2:2 + 2 * twos:2].set(receiver + moved)
    return tallies[jax.random.permutation(jax.random.fold_in(own_key, 2), amount)]


def setup_inputs(seed: int = 0) -> dict:
    streams_of = jax.random.split(jax.random.key(seed), 5)
    boxes = draw_boxes(jax.random.fold_in(streams_of[4], 71), 0)
    prototypes = draw_prototypes(jax.random.fold_in(streams_of[4], 71), 0)
    counts = jax.vmap(lambda own: ragged_sizes(own, IMG_DEV, LIVE, BOXES, 2))(jax.random.split(streams_of[2], GROUPS)).reshape((GROUPS, IMG_DEV)).astype(jnp.int32)
    keep = set_ends((jax.random.randint(streams_of[3], (IMAGES, BOXES), 0, 4) < 3).astype(jnp.int32), jax.random.fold_in(streams_of[3], 1), 0, 1)
    return dict(boxes=boxes, prototypes=prototypes, counts=counts, keep=keep)


def reference(boxes, prototypes, counts, keep):
    flat_rows = boxes.reshape(IMAGES * BOXES, D)
    slot_iota = lax.broadcasted_iota(jnp.int32, (IMAGES, BOXES), 1)
    is_live = ((keep == 1) & (slot_iota < counts.reshape(IMAGES, 1))).reshape(IMAGES * BOXES)
    blocks = prototypes.reshape(N_BANK, VDEV, D)

    def block_peak(block):
        scores = lax.dot_general(flat_rows, block, (((1,), (1,)), ((), ())), preferred_element_type=jnp.float32)
        return jnp.max(scores, axis=1)

    row_peak = jnp.max(lax.map(block_peak, blocks), axis=0)

    def accumulate(carry, block):
        scores = lax.dot_general(flat_rows, block, (((1,), (1,)), ((), ())), preferred_element_type=jnp.float32)
        exponent = jnp.exp(scores - row_peak[:, None])
        new_mass = carry[0] + jnp.sum(exponent, axis=1)
        new_pull = carry[1] + jnp.dot(exponent.astype(jnp.bfloat16), block, preferred_element_type=jnp.float32)
        return (new_mass, new_pull), None

    start = (jnp.zeros((IMAGES * BOXES,), jnp.float32), jnp.zeros((IMAGES * BOXES, D), jnp.float32))
    (row_mass, row_pull), _ = lax.scan(accumulate, start, blocks)
    confidence = -jnp.log(row_mass)
    conf_sum = jnp.sum(jnp.where(is_live, confidence, 0.0))
    conf_count = jnp.sum(is_live.astype(jnp.float32))
    mean_conf = conf_sum / jnp.maximum(conf_count, 1.0)
    log_norm = jnp.where(is_live, row_peak + jnp.log(row_mass), 0.0)
    top_logprob = jnp.where(is_live, confidence - mean_conf, 0.0)
    targets = jnp.where(is_live[:, None], row_pull / row_mass[:, None], 0.0).astype(jnp.bfloat16)
    return (targets.reshape(IMAGES, BOXES, D), top_logprob.reshape(IMAGES, BOXES), log_norm.reshape(IMAGES, BOXES))
```

```python
import functools

import jax
import jax.numpy as jnp
from jax import lax
from jax.experimental import pallas as pl
from jax.experimental.pallas import tpu as pltpu
from jax.sharding import PartitionSpec as P

LIVE = 320
F32 = jnp.float32
BF16 = jnp.bfloat16
TILE = 2048
PIECE = 512


class Plan:
    def __init__(self, boxes, banks):
        self.boxes, self.banks = boxes, banks
        self.share = boxes // banks
        self.half = LIVE // 2
        self.base = LIVE - boxes
        self.flex = boxes - self.half
        self.zs = banks // 2
        self.long_blocks = self.half // self.share
        self.base_blocks = self.base // self.share
        self.short_per = (self.long_blocks + 1) // 2
        self.blocks = self.zs + self.short_per
        self.rows = self.blocks * self.share

    def short_row(self, owner):
        owner = jnp.minimum(owner, self.long_blocks - 1)
        return jnp.where(
            owner < self.base_blocks,
            self.boxes + self.share * owner,
            self.half + self.share * (self.long_blocks - 1 - owner),
        )

    def block_row(self, q, x):
        if q < self.zs:
            return self.share * (2 * q + x)
        return self.short_row(2 * (q - self.zs) + x)


def iota(shape, axis):
    return lax.broadcasted_iota(jnp.int32, shape, axis)


def long_image(cnt_ref):
    return jnp.where(cnt_ref[0, 1] > cnt_ref[0, 0], 1, 0)


def bank_kernel(plan, cols, cnt_hbm, pos_ref, boxes_hbm, keep_hbm, bank_hbm, *rest):
    stat_ref = rest[0]
    chunks = (len(rest) - 11) // 2
    outs = rest[1:1 + 2 * chunks]
    cnt_ref, boxes_ref, keep_ref, x_v, bank_v, s_v, acc_v, small_sems, box_sem, sems = rest[1 + 2 * chunks:]
    small = (pltpu.make_async_copy(cnt_hbm, cnt_ref, small_sems.at[0]),
             pltpu.make_async_copy(keep_hbm, keep_ref, small_sems.at[1]),
             pltpu.make_async_copy(boxes_hbm, boxes_ref, box_sem))
    for copy in small:
        copy.start()
    bank = bank_v.shape[0]
    tile = min(TILE, bank)

    def piece(i):
        rows = pl.ds(i * PIECE, PIECE)
        return pltpu.make_async_copy(bank_hbm.at[rows], bank_v.at[rows], sems.at[i])

    for i in range(bank // PIECE):
        piece(i).start()
    for copy in small:
        copy.wait()
    half, base, boxes, flex = plan.half, plan.base, plan.boxes, plan.flex
    li = long_image(cnt_ref)
    si = 1 - li
    extra = cnt_ref[0, li] - half
    flip = (iota((flex, flex), 0) + iota((flex, flex), 1) == flex - 1).astype(BF16)
    back = jnp.dot(flip, boxes_ref[si, base:half, :], preferred_element_type=F32)
    front = boxes_ref[li, half:boxes, :].astype(F32)
    x_v[0:half, :] = boxes_ref[li, 0:half, :]
    x_v[half:boxes, :] = jnp.where(iota(front.shape, 0) < extra, front, back).astype(BF16)
    x_v[boxes:LIVE, :] = boxes_ref[si, 0:base, :]

    def scores(i, top):
        for k in range(tile // PIECE):
            piece(i * (tile // PIECE) + k).wait()
        s = lax.dot_general(x_v[...], bank_v[pl.ds(i * tile, tile)], (((1,), (1,)), ((), ())),
                            preferred_element_type=F32)
        s_v[i] = s
        for j in range(tile // 128):
            top = jnp.maximum(top, s[:, j * 128:(j + 1) * 128])
        return top

    top = lax.fori_loop(0, bank // tile, scores, jnp.full((LIVE, 128), -jnp.inf, F32))
    peak = jnp.max(top, axis=1, keepdims=True)
    acc_v[...] = jnp.zeros_like(acc_v)

    def pulls(i, mass):
        e = jnp.exp(s_v[i] - peak)
        for j in range(tile // 128):
            mass = mass + e[:, j * 128:(j + 1) * 128]
        acc_v[...] += jnp.dot(e.astype(BF16), bank_v[pl.ds(i * tile, tile)],
                              preferred_element_type=F32)
        return mass

    mass = lax.fori_loop(0, bank // tile, pulls, jnp.zeros((LIVE, 128), F32))
    mass = jnp.sum(mass, axis=1, keepdims=True)
    both = jnp.where(iota((LIVE, 128), 1) == 0, peak, mass)
    lanes = jnp.transpose(both)[0:8, :]
    keep_l = (keep_ref[pl.ds(li, 1), :] == 1).astype(F32)
    keep_s = (keep_ref[pl.ds(si, 1), :] == 1).astype(F32)
    turn = (iota((boxes, boxes), 0) + iota((boxes, boxes), 1) == LIVE - 1).astype(BF16)
    turned = jnp.dot(jnp.broadcast_to(keep_s, (8, boxes)).astype(BF16), turn,
                     preferred_element_type=F32)[0:1, :]
    lane = iota((1, boxes), 1)
    live_long = jnp.where(lane < half + extra, keep_l, turned)
    live_short = jnp.where(lane < base, keep_s, 0.0)
    pad = jnp.zeros((1, 2 * boxes - LIVE), F32)
    packed = jnp.concatenate([
        lanes[0:1, 0:boxes],
        jnp.concatenate([lanes[0:1, boxes:LIVE], pad], axis=1),
        lanes[1:2, 0:boxes],
        jnp.concatenate([lanes[1:2, boxes:LIVE], pad], axis=1),
        live_long, live_short, live_long, live_short], axis=0)
    stat_ref[...] = packed
    outs[0][plan.rows:plan.rows + 8, :] = packed
    x = pos_ref[0] % 2
    for q in range(plan.blocks):
        out = pl.ds(q * plan.share, plan.share)
        for kind, which in ((0, 1 - x), (1, x)):
            src = pl.ds(pl.multiple_of(plan.block_row(q, which), 8), plan.share)
            for c in range(chunks):
                outs[2 * c + kind][out, :] = acc_v[src, c * cols:(c + 1) * cols]


def merge_stats(tiles):
    peak = functools.reduce(jnp.maximum, [t[0:2, :] for t in tiles])
    factors = [jnp.exp(t[0:2, :] - peak) for t in tiles]
    mass = functools.reduce(jnp.add, [t[2:4, :] * f for t, f in zip(tiles, factors)])
    return peak, factors, mass


def store_columns(plan, values, col_ref):
    width = plan.boxes
    fill = [jnp.zeros((1, width), F32)] * (8 - len(values))
    top = jnp.transpose(jnp.concatenate([v[0:1, :] for v in values] + fill, axis=0))
    low = jnp.transpose(jnp.concatenate([v[1:2, :] for v in values] + fill, axis=0))
    col_ref[0:width, :] = top
    col_ref[width:LIVE, :] = low[0:LIVE - width, :]


def pair_kernel(plan, has_tile, pos_ref, own_ref, got_ref, mine_ref, theirs_ref, *rest):
    outs, col_v = rest[:-1], rest[-1]
    x, z = pos_ref[0] % 2, pos_ref[0] // 2
    mine, theirs = mine_ref[...], theirs_ref[...]
    peak, factors, mass = merge_stats([mine, theirs])
    store_columns(plan, factors, col_v)
    share = plan.share
    for s in range(plan.zs):
        to = z ^ s
        q_short = plan.zs + jnp.minimum(to, plan.short_per - 1)
        owner = 2 * to + x
        for at, q, row in ((0, to, share * owner), (share, q_short, plan.short_row(owner))):
            src = pl.ds(pl.multiple_of(q * share, 8), share)
            col = col_v[pl.ds(pl.multiple_of(row, 8), share), :]
            outs[s][at:at + share, :] = own_ref[src, :] * col[:, 0:1] + got_ref[src, :] * col[:, 1:2]
        if has_tile:
            outs[s][2 * share:2 * share + 8, :] = jnp.concatenate([peak, mass, mine[4:8, :]], axis=0)


def conf_kernel(plan, *refs):
    out_ref = refs[-1]
    tiles = [r[2 * plan.share:2 * plan.share + 8, :] for r in refs[:-1]]
    _, _, mass = merge_stats(tiles)
    live = tiles[0][4:6, :]
    row = jnp.where(live > 0.5, -jnp.log(jnp.where(live > 0.5, mass, 1.0)), 0.0)
    total, count = jnp.sum(row), jnp.sum(live)
    out_ref[...] = jnp.where(iota((8, 128), 0) == 0, total, count)


def final_kernel(plan, chunks, images, cnt_ref, pos_ref, keep_ref, *refs):
    zs, share = plan.zs, plan.share
    confs = refs[:images]
    pulls = refs[images:images + zs * chunks]
    out_ref, prob_ref, norm_ref, col_v = refs[images + zs * chunks:]
    me = pos_ref[0]
    li = long_image(cnt_ref)
    si = 1 - li
    tiles = [pulls[s][2 * share:2 * share + 8, :] for s in range(zs)]
    peak, factors, mass = merge_stats(tiles)
    conf = functools.reduce(jnp.add, [c[...] for c in confs])
    mean = conf[0:1, 0:1] / jnp.maximum(conf[1:2, 0:1], 1.0)

    lane = iota((plan.boxes, 128), 1)
    src = iota((plan.boxes, 128), 0)
    slot = share * me + lane
    is_base = me < plan.base_blocks
    long_pick = (src == slot).astype(F32)
    short_pick = (src == jnp.where(is_base, slot, LIVE - 1 - slot)).astype(F32)
    stack = jnp.concatenate([peak, jnp.log(jnp.where(mass > 0.0, mass, 1.0)), mass, peak], axis=0)
    pick = functools.partial(jnp.dot, preferred_element_type=F32, precision=lax.Precision.HIGHEST)
    long_vals = pick(stack, long_pick)
    short_vals = pick(stack, short_pick)
    short_vals = jnp.where(is_base, pltpu.roll(short_vals, 7, 0), short_vals)
    keep = (keep_ref[...] == 1).astype(F32)
    keep_own = pick(jnp.concatenate([keep] * 4, axis=0), long_pick)
    slot_row = share * me + iota((1, 128), 1)
    live_rows = []
    for image, vals in ((li, long_vals), (si, short_vals)):
        kept = jnp.where(image == 0, keep_own[0:1, :], keep_own[1:2, :])
        live = (kept > 0.5) & (slot_row < cnt_ref[0, image])
        live_rows.append(live.astype(F32))
        norm = jnp.where(live, vals[0:1, :] + vals[2:3, :], 0.0)
        prob = jnp.where(live, -vals[2:3, :] - mean, 0.0)
        norm_ref[pl.ds(image, 1), :] = norm[:, 0:share]
        prob_ref[pl.ds(image, 1), :] = prob[:, 0:share]
    live_cols = jnp.transpose(jnp.concatenate(live_rows + [jnp.zeros((6, 128), F32)], axis=0))

    width = pulls[0].shape[1]
    for part in range(0, zs, 6):
        group = range(part, min(part + 6, zs))
        store_columns(plan, [factors[s] for s in group] + [mass], col_v.at[part // 6])
    rows = (share * me, plan.short_row(me))
    turned = (me >= plan.base_blocks) & (me < plan.long_blocks)
    for which, image in ((0, li), (1, si)):
        at = which * share
        col = [col_v[p, pl.ds(pl.multiple_of(rows[which], 8), share), :] for p in range(col_v.shape[0])]
        n_last = min(6, zs)
        m = col[0][:, n_last:n_last + 1]
        live = live_cols[0:share, which:which + 1] > 0.5
        for c in range(chunks):
            total = jnp.zeros((share, width), F32)
            for s in range(zs):
                total = total + pulls[c * zs + s][at:at + share, :] * col[s // 6][:, s % 6:s % 6 + 1]
            value = (total / m).astype(BF16)
            if which == 1:
                a, b = iota((share, share), 0), iota((share, share), 1)
                order = (b == jnp.where(turned, share - 1 - a, a)).astype(BF16)
                value = jnp.dot(order, value, preferred_element_type=F32).astype(BF16)
            value = jnp.where(live, value, jnp.zeros_like(value))
            out_ref[image, :, c * width:(c + 1) * width] = value


VM = pl.BlockSpec(memory_space=pltpu.VMEM)
SM = pl.BlockSpec(memory_space=pltpu.SMEM)
ANY = pl.BlockSpec(memory_space=pl.ANY)
MIB = 2**20


def call(body, ins, outs, scratch, flops, moved, limit, out_specs=None):
    return pl.pallas_call(
        body,
        out_shape=[jax.ShapeDtypeStruct(shape, dtype) for shape, dtype in outs],
        in_specs=ins,
        out_specs=out_specs or [VM] * len(outs),
        scratch_shapes=scratch,
        compiler_params=pltpu.CompilerParams(vmem_limit_bytes=limit * MIB),
        cost_estimate=pl.CostEstimate(flops=flops, bytes_accessed=moved, transcendentals=0),
    )


def on_device(boxes, prototypes, counts, keep):
    images, slots, width = boxes.shape
    bank = prototypes.shape[0]
    banks = lax.axis_size("bank")
    groups = lax.axis_size("img")
    plan = Plan(slots, banks)
    zs, share = plan.zs, plan.share
    pos = lax.axis_index("bank").reshape(1)
    cols = slots
    chunks = width // cols
    high = [plan.rows + (8 if c == 0 else 0) for c in range(chunks)]
    outs = call(
        functools.partial(bank_kernel, plan, cols),
        [ANY, SM, ANY, ANY, ANY],
        [((8, slots), F32)] + [((h, cols), F32) for c in range(chunks) for h in (high[c], plan.rows)],
        [pltpu.SMEM(counts.shape, jnp.int32), pltpu.VMEM(boxes.shape, BF16),
         pltpu.VMEM(keep.shape, jnp.int32), pltpu.VMEM((LIVE, width), BF16),
         pltpu.VMEM((bank, width), BF16), pltpu.VMEM((bank // TILE, LIVE, TILE), F32),
         pltpu.VMEM((LIVE, width), F32), pltpu.SemaphoreType.DMA((2,)), pltpu.SemaphoreType.DMA,
         pltpu.SemaphoreType.DMA((bank // PIECE,))],
        4 * LIVE * bank * width, bank * width * 2, 40,
    )(counts, pos, boxes, keep, prototypes)
    stat, sends, owns = outs[0], outs[1::2], outs[2::2]

    pair = [(i, i ^ 1) for i in range(banks)]
    theirs = None
    pulls = []
    for c in range(chunks):
        got = lax.ppermute(sends[c], "bank", pair)
        theirs = got[plan.rows:] if c == 0 else theirs
        tall = 2 * share + (8 if c == 0 else 0)
        outs = call(
            functools.partial(pair_kernel, plan, c == 0),
            [SM, VM, VM, VM, VM],
            [((tall, cols), F32)] * zs,
            [pltpu.VMEM((LIVE, 8), F32)],
            plan.rows * cols * 4, plan.rows * cols * 16, 8,
        )(pos, owns[c], got, stat, theirs)
        moved = [lax.ppermute(outs[s], "bank", [(i, i ^ (2 * s)) for i in range(banks)])
                 for s in range(1, zs)]
        pulls.append([outs[0]] + moved)

    conf, = call(functools.partial(conf_kernel, plan), [VM] * zs, [((8, 128), F32)], [],
                 slots * 8, slots * 64, 4)(*pulls[0])
    confs = [conf] + [lax.ppermute(conf, "img", [(i, i ^ s) for i in range(groups)])
                      for s in range(1, groups)]
    targets, top_logprob, log_norm = call(
        functools.partial(final_kernel, plan, chunks, groups),
        [SM, SM, VM] + [VM] * (groups + zs * chunks),
        [((images, share, width), BF16), ((images, share), F32), ((images, share), F32)],
        [pltpu.VMEM(((zs + 5) // 6, LIVE, 8), F32)],
        zs * share * width * 4, zs * share * width * 8, 16,
    )(counts, pos, keep, *confs, *[p for group in pulls for p in group])
    return targets, top_logprob, log_norm


def solution(mesh):
    placed = (P("img", None, None), P("bank", None), P("img", None), P("img", None))
    return jax.shard_map(
        on_device,
        mesh=mesh,
        in_specs=placed,
        out_specs=(P("img", "bank", None), P("img", "bank"), P("img", "bank")),
        check_vma=False,
    )
```

```python
import functools

import jax
import jax.numpy as jnp
from jax import lax
from jax.experimental import pallas as pl
from jax.experimental.pallas import tpu as pltpu
from jax.sharding import PartitionSpec as P

LIVE = 320
F32 = jnp.float32
BF16 = jnp.bfloat16
TILE = 2048
PIECE = 512


class Plan:
    def __init__(self, boxes, banks):
        self.boxes, self.banks = boxes, banks
        self.share = boxes // banks
        self.half = LIVE // 2
        self.base = LIVE - boxes
        self.flex = boxes - self.half
        self.near = 4
        self.far = banks // self.near
        self.long_blocks = self.half // self.share
        self.base_blocks = self.base // self.share
        self.short_far = -(-self.long_blocks // self.near)
        self.short_half = [sum(self.half_owner(b, i, 0) < self.long_blocks for i in range(banks // 2))
                           for b in (0, 1)]

    def half_owner(self, bit, i, value):
        if bit == 0:
            return 2 * i + value
        return i // 2 * 4 + 2 * value + i % 2

    def half_index(self, bit, owner):
        return owner // 2 if bit == 0 else owner // 4 * 2 + owner % 2

    def half_rows(self, bit):
        return self.share * (self.banks // 2 + self.short_half[bit])

    def half_blocks(self, bit, value):
        own = [self.half_owner(bit, i, value) for i in range(self.banks // 2)]
        return [self.share * o for o in own] + [self.short_row(o) for o in own[:self.short_half[bit]]]

    def quarter_rows(self):
        return self.share * (self.far + self.short_far)

    def quarter_picks(self, bit, me):
        lists = []
        for low in (me % 4, me % 4 ^ (2 >> bit)):
            picks = []
            for h in range(self.far):
                owner = self.near * h + low
                picks.append((self.half_index(bit, owner), self.share * owner))
            for h in range(self.short_far):
                owner = self.near * h + low
                q = jnp.minimum(self.half_index(bit, owner), self.short_half[bit] - 1)
                picks.append((self.banks // 2 + q, self.short_row(owner)))
            lists.append(picks)
        return lists

    def own_picks(self, me):
        lists = []
        for s in range(self.far):
            to = me // 4 ^ s
            owner = self.near * to + me % 4
            q = self.far + jnp.minimum(to, self.short_far - 1)
            lists.append([(to, self.share * owner), (q, self.short_row(owner))])
        return lists

    def short_row(self, owner):
        owner = jnp.minimum(owner, self.long_blocks - 1)
        return jnp.where(
            owner < self.base_blocks,
            self.boxes + self.share * owner,
            self.half + self.share * (self.long_blocks - 1 - owner),
        )


def iota(shape, axis):
    return lax.broadcasted_iota(jnp.int32, shape, axis)


def long_image(cnt_ref):
    return jnp.where(cnt_ref[0, 1] > cnt_ref[0, 0], 1, 0)


def bank_kernel(plan, cols, firsts, carry, cnt_ref, pos_ref, boxes_hbm, bank_hbm, *rest):
    stat_ref = rest[0]
    chunks = len(firsts)
    outs = rest[1:1 + 2 * chunks]
    boxes_ref, x_v, bank_v, s_v, acc_v, box_sem, sems = rest[1 + 2 * chunks:]
    box_copy = pltpu.make_async_copy(boxes_hbm, boxes_ref, box_sem)
    box_copy.start()
    bank = bank_v.shape[0]
    tile = min(TILE, bank)

    def piece(i):
        rows = pl.ds(i * PIECE, PIECE)
        return pltpu.make_async_copy(bank_hbm.at[rows], bank_v.at[rows], sems.at[i])

    per = tile // PIECE
    for i in range(per):
        piece(i).start()
    box_copy.wait()
    half, base, boxes, flex = plan.half, plan.base, plan.boxes, plan.flex
    li = long_image(cnt_ref)
    si = 1 - li
    extra = cnt_ref[0, li] - half
    flip = (iota((flex, flex), 0) + iota((flex, flex), 1) == flex - 1).astype(BF16)
    back = jnp.dot(flip, boxes_ref[si, base:half, :], preferred_element_type=F32)
    front = boxes_ref[li, half:boxes, :].astype(F32)
    x_v[0:half, :] = boxes_ref[li, 0:half, :]
    x_v[half:boxes, :] = jnp.where(iota(front.shape, 0) < extra, front, back).astype(BF16)
    x_v[boxes:LIVE, :] = boxes_ref[si, 0:base, :]
    for i in range(per, min(2 * per, bank // PIECE)):
        piece(i).start()

    def scores(i, top):
        for k in range(per):
            piece(i * per + k).wait()

        @pl.when(i + 2 < bank // tile)
        def _():
            for k in range(per):
                piece((i + 2) * per + k).start()

        s = lax.dot_general(x_v[...], bank_v[pl.ds(i * tile, tile)], (((1,), (1,)), ((), ())),
                            preferred_element_type=F32)
        s_v[i] = s
        for j in range(tile // 128):
            top = jnp.maximum(top, s[:, j * 128:(j + 1) * 128])
        return top

    top = lax.fori_loop(0, bank // tile, scores, jnp.full((LIVE, 128), -jnp.inf, F32))
    peak = jnp.max(top, axis=1, keepdims=True)
    acc_v[...] = jnp.zeros_like(acc_v)

    def pulls(i, mass):
        e = jnp.exp(s_v[i] - peak)
        for j in range(tile // 128):
            mass = mass + e[:, j * 128:(j + 1) * 128]
        acc_v[...] += jnp.dot(e.astype(BF16), bank_v[pl.ds(i * tile, tile)],
                              preferred_element_type=F32)
        return mass

    mass = lax.fori_loop(0, bank // tile, pulls, jnp.zeros((LIVE, 128), F32))
    mass = jnp.sum(mass, axis=1, keepdims=True)
    both = jnp.where(iota((LIVE, 128), 1) == 0, peak, mass)
    lanes = jnp.transpose(both)[0:8, :]
    pad = jnp.zeros((1, 2 * boxes - LIVE), F32)
    packed = jnp.concatenate([
        lanes[0:1, 0:boxes],
        jnp.concatenate([lanes[0:1, boxes:LIVE], pad], axis=1),
        lanes[1:2, 0:boxes],
        jnp.concatenate([lanes[1:2, boxes:LIVE], pad], axis=1),
        jnp.zeros((4, boxes), F32)], axis=0)
    stat_ref[...] = packed
    share = plan.share
    for c, bit in enumerate(firsts):
        mine = pos_ref[0] // (1 << bit) % 2
        if carry[c]:
            rows = plan.half_rows(bit)
            outs[2 * c + 1][rows:rows + 8, :] = packed
        for kind, value in ((0, mine), (1, 1 - mine)):
            for q, row in enumerate(plan.half_blocks(bit, value)):
                outs[2 * c + kind][q * share:(q + 1) * share, :] = acc_v[
                    pl.ds(pl.multiple_of(row, 8), share), c * cols:(c + 1) * cols]


def merge_stats(tiles):
    peak = functools.reduce(jnp.maximum, [t[0:2, :] for t in tiles])
    factors = [jnp.exp(t[0:2, :] - peak) for t in tiles]
    mass = functools.reduce(jnp.add, [t[2:4, :] * f for t, f in zip(tiles, factors)])
    return peak, factors, mass


def store_columns(plan, values, col_ref):
    width = plan.boxes
    fill = [jnp.zeros((1, width), F32)] * (8 - len(values))
    top = jnp.transpose(jnp.concatenate([v[0:1, :] for v in values] + fill, axis=0))
    low = jnp.transpose(jnp.concatenate([v[1:2, :] for v in values] + fill, axis=0))
    col_ref[0:width, :] = top
    col_ref[width:LIVE, :] = low[0:LIVE - width, :]


def merge_kernel(plan, picks, has_tile, pos_ref, own_ref, got_ref, mine_ref, theirs_ref, *rest):
    outs, col_v = rest[:-1], rest[-1]
    share = plan.share
    peak, factors, mass = merge_stats([mine_ref[...], theirs_ref[...]])
    store_columns(plan, factors, col_v)
    for out_ref, blocks in zip(outs, picks(pos_ref[0])):
        for at, (q, row) in enumerate(blocks):
            src = pl.ds(pl.multiple_of(q * share, 8), share)
            col = col_v[pl.ds(pl.multiple_of(row, 8), share), :]
            out_ref[at * share:(at + 1) * share, :] = (
                own_ref[src, :] * col[:, 0:1] + got_ref[src, :] * col[:, 1:2])
        if has_tile:
            end = len(blocks) * share
            out_ref[end:end + 8, :] = jnp.concatenate([peak, mass, peak, mass], axis=0)


def conf_kernel(plan, cnt_ref, keep_ref, *refs):
    out_ref = refs[-1]
    half, base, boxes = plan.half, plan.base, plan.boxes
    li = long_image(cnt_ref)
    keep_l = (keep_ref[pl.ds(li, 1), :] == 1).astype(F32)
    keep_s = (keep_ref[pl.ds(1 - li, 1), :] == 1).astype(F32)
    turn = (iota((boxes, boxes), 0) + iota((boxes, boxes), 1) == LIVE - 1).astype(BF16)
    turned = jnp.dot(jnp.broadcast_to(keep_s, (8, boxes)).astype(BF16), turn,
                     preferred_element_type=F32)[0:1, :]
    lane = iota((1, boxes), 1)
    live = jnp.concatenate([jnp.where(lane < cnt_ref[0, li], keep_l, turned),
                            jnp.where(lane < base, keep_s, 0.0)], axis=0)
    tiles = [r[2 * plan.share:2 * plan.share + 8, :] for r in refs[:-1]]
    _, _, mass = merge_stats(tiles)
    row = jnp.where(live > 0.5, -jnp.log(jnp.where(live > 0.5, mass, 1.0)), 0.0)
    total, count = jnp.sum(row), jnp.sum(live)
    out_ref[...] = jnp.where(iota((8, 128), 0) == 0, total, count)


def final_kernel(plan, chunks, images, cnt_ref, pos_ref, keep_ref, *refs):
    zs, share = plan.far, plan.share
    confs = refs[:images]
    pulls = refs[images:images + zs * chunks]
    out_ref, prob_ref, norm_ref, col_v = refs[images + zs * chunks:]
    me = pos_ref[0]
    li = long_image(cnt_ref)
    si = 1 - li
    tiles = [pulls[s][2 * share:2 * share + 8, :] for s in range(zs)]
    peak, factors, mass = merge_stats(tiles)
    conf = functools.reduce(jnp.add, [c[...] for c in confs])
    mean = conf[0:1, 0:1] / jnp.maximum(conf[1:2, 0:1], 1.0)

    lane = iota((plan.boxes, 128), 1)
    src = iota((plan.boxes, 128), 0)
    slot = share * me + lane
    is_base = me < plan.base_blocks
    long_pick = (src == slot).astype(F32)
    short_pick = (src == jnp.where(is_base, slot, LIVE - 1 - slot)).astype(F32)
    stack = jnp.concatenate([peak, jnp.log(jnp.where(mass > 0.0, mass, 1.0)), mass, peak], axis=0)
    pick = functools.partial(jnp.dot, preferred_element_type=F32, precision=lax.Precision.HIGHEST)
    long_vals = pick(stack, long_pick)
    short_vals = pick(stack, short_pick)
    short_vals = jnp.where(is_base, pltpu.roll(short_vals, 7, 0), short_vals)
    keep = (keep_ref[...] == 1).astype(F32)
    keep_own = pick(jnp.concatenate([keep] * 4, axis=0), long_pick)
    slot_row = share * me + iota((1, 128), 1)
    live_rows = []
    for image, vals in ((li, long_vals), (si, short_vals)):
        kept = jnp.where(image == 0, keep_own[0:1, :], keep_own[1:2, :])
        live = (kept > 0.5) & (slot_row < cnt_ref[0, image])
        live_rows.append(live.astype(F32))
        norm = jnp.where(live, vals[0:1, :] + vals[2:3, :], 0.0)
        prob = jnp.where(live, -vals[2:3, :] - mean, 0.0)
        norm_ref[pl.ds(image, 1), :] = norm[:, 0:share]
        prob_ref[pl.ds(image, 1), :] = prob[:, 0:share]
    live_cols = jnp.transpose(jnp.concatenate(live_rows + [jnp.zeros((6, 128), F32)], axis=0))

    width = pulls[0].shape[1]
    for part in range(0, zs, 6):
        group = range(part, min(part + 6, zs))
        store_columns(plan, [factors[s] for s in group] + [mass], col_v.at[part // 6])
    rows = (share * me, plan.short_row(me))
    turned = (me >= plan.base_blocks) & (me < plan.long_blocks)
    for which, image in ((0, li), (1, si)):
        at = which * share
        col = [col_v[p, pl.ds(pl.multiple_of(rows[which], 8), share), :] for p in range(col_v.shape[0])]
        n_last = min(6, zs)
        m = col[0][:, n_last:n_last + 1]
        live = live_cols[0:share, which:which + 1] > 0.5
        for c in range(chunks):
            total = jnp.zeros((share, width), F32)
            for s in range(zs):
                total = total + pulls[c * zs + s][at:at + share, :] * col[s // 6][:, s % 6:s % 6 + 1]
            value = (total / m).astype(BF16)
            if which == 1:
                a, b = iota((share, share), 0), iota((share, share), 1)
                order = (b == jnp.where(turned, share - 1 - a, a)).astype(BF16)
                value = jnp.dot(order, value, preferred_element_type=F32).astype(BF16)
            value = jnp.where(live, value, jnp.zeros_like(value))
            out_ref[image, :, c * width:(c + 1) * width] = value


VM = pl.BlockSpec(memory_space=pltpu.VMEM)
SM = pl.BlockSpec(memory_space=pltpu.SMEM)
HBM = pl.BlockSpec(memory_space=pltpu.HBM)
MIB = 2**20
VMEM_MIB = 52
FIRST_BIT = (0, 1, 0)


def call(body, ins, outs, scratch, flops, moved, limit, out_specs=None):
    return pl.pallas_call(
        body,
        out_shape=[jax.ShapeDtypeStruct(shape, dtype) for shape, dtype in outs],
        in_specs=ins,
        out_specs=out_specs or [VM] * len(outs),
        scratch_shapes=scratch,
        compiler_params=pltpu.CompilerParams(vmem_limit_bytes=limit * MIB),
        cost_estimate=pl.CostEstimate(flops=flops, bytes_accessed=moved, transcendentals=0),
    )


def on_device(boxes, prototypes, counts, keep):
    images, slots, width = boxes.shape
    bank = prototypes.shape[0]
    banks = lax.axis_size("bank")
    groups = lax.axis_size("img")
    plan = Plan(slots, banks)
    near, far, share = plan.near, plan.far, plan.share
    pos = lax.axis_index("bank").reshape(1)
    cols = slots
    chunks = width // cols
    firsts = [FIRST_BIT[c % len(FIRST_BIT)] for c in range(chunks)]
    carry = [bit not in firsts[:c] for c, bit in enumerate(firsts)]
    shapes = [((8, slots), F32)]
    for c in range(chunks):
        rows = plan.half_rows(firsts[c])
        shapes += [((rows, cols), F32), ((rows + 8 * carry[c], cols), F32)]
    stat, *parts = call(
        functools.partial(bank_kernel, plan, cols, firsts, carry),
        [SM, SM, HBM, HBM],
        shapes,
        [pltpu.VMEM(boxes.shape, BF16), pltpu.VMEM((LIVE, width), BF16),
         pltpu.VMEM((bank, width), BF16), pltpu.VMEM((bank // TILE, LIVE, TILE), F32),
         pltpu.VMEM((LIVE, width), F32), pltpu.SemaphoreType.DMA,
         pltpu.SemaphoreType.DMA((bank // PIECE,))],
        4 * LIVE * bank * width, bank * width * 2, VMEM_MIB,
    )(counts, pos, boxes, prototypes)

    def swap(array, step):
        return lax.ppermute(array, "bank", [(i, i ^ step) for i in range(banks)])

    def merge(picks, number, rows, has_tile, *arrays):
        return call(
            functools.partial(merge_kernel, plan, picks, has_tile),
            [SM] + [VM] * 4, [((rows + 8 * has_tile, cols), F32)] * number,
            [pltpu.VMEM((LIVE, 8), F32)],
            number * rows * cols * 4, number * rows * cols * 16, 8,
        )(pos, *arrays)

    got = [swap(parts[2 * c + 1], 1 << firsts[c]) for c in range(chunks)]
    first_tile = {firsts[c]: got[c][plan.half_rows(firsts[c]):] for c in range(chunks) if carry[c]}
    quarters = plan.quarter_rows()
    second_tiles = {}
    second = []
    for c, bit in enumerate(firsts):
        own, send = merge(functools.partial(plan.quarter_picks, bit), 2, quarters, carry[c],
                          parts[2 * c], got[c], stat, first_tile[bit])
        second.append((own, swap(send, 2 >> bit)))
        if carry[c]:
            second_tiles[bit] = (own[quarters:], second[c][1][quarters:])
    pulls = []
    for c, bit in enumerate(firsts):
        outs = merge(plan.own_picks, far, 2 * share, c == 0, *second[c], *second_tiles[bit])
        pulls.append([outs[0]] + [swap(outs[s], near * s) for s in range(1, far)])

    conf, = call(functools.partial(conf_kernel, plan), [SM, VM] + [VM] * far, [((8, 128), F32)], [],
                 slots * 8, slots * 64, 4)(counts, keep, *pulls[0])
    confs = [conf] + [lax.ppermute(conf, "img", [(i, i ^ s) for i in range(groups)])
                      for s in range(1, groups)]
    targets, top_logprob, log_norm = call(
        functools.partial(final_kernel, plan, chunks, groups),
        [SM, SM, VM] + [VM] * (groups + far * chunks),
        [((images, share, width), BF16), ((images, share), F32), ((images, share), F32)],
        [pltpu.VMEM(((far + 5) // 6, LIVE, 8), F32)],
        far * share * width * 4, far * share * width * 8, 16,
    )(counts, pos, keep, *confs, *[p for group in pulls for p in group])
    return targets, top_logprob, log_norm


def solution(mesh):
    placed = (P("img", None, None), P("bank", None), P("img", None), P("img", None))
    return jax.shard_map(
        on_device,
        mesh=mesh,
        in_specs=placed,
        out_specs=(P("img", "bank", None), P("img", "bank"), P("img", "bank")),
        check_vma=False,
    )
```

```python
import functools

import jax
import jax.numpy as jnp
from jax import lax
from jax.experimental import pallas as pl
from jax.experimental.pallas import tpu as pltpu
from jax.sharding import PartitionSpec as P


LIVE = 320
F32 = jnp.float32
BF16 = jnp.bfloat16
TILE = 2048
PIECE = 512


class Plan:
    def __init__(self, boxes, banks):
        self.boxes, self.banks = boxes, banks
        self.share = boxes // banks
        self.half = LIVE // 2
        self.base = LIVE - boxes
        self.flex = boxes - self.half
        self.near = 4
        self.far = banks // self.near
        self.long_blocks = self.half // self.share
        self.base_blocks = self.base // self.share
        self.short_far = -(-self.long_blocks // self.near)
        self.short_half = [sum(self.half_owner(b, i, 0) < self.long_blocks for i in range(banks // 2))
                           for b in (0, 1)]

    def half_owner(self, bit, i, value):
        if bit == 0:
            return 2 * i + value
        return i // 2 * 4 + 2 * value + i % 2

    def half_index(self, bit, owner):
        return owner // 2 if bit == 0 else owner // 4 * 2 + owner % 2

    def half_rows(self, bit):
        return self.share * (self.banks // 2 + self.short_half[bit])

    def half_blocks(self, bit, value):
        own = [self.half_owner(bit, i, value) for i in range(self.banks // 2)]
        return [self.share * o for o in own] + [self.short_row(o) for o in own[:self.short_half[bit]]]

    def quarter_rows(self):
        return self.share * (self.far + self.short_far)

    def quarter_picks(self, bit, me):
        lists = []
        for low in (me % 4, me % 4 ^ (2 >> bit)):
            picks = []
            for h in range(self.far):
                owner = self.near * h + low
                picks.append((self.half_index(bit, owner), self.share * owner))
            for h in range(self.short_far):
                owner = self.near * h + low
                q = jnp.minimum(self.half_index(bit, owner), self.short_half[bit] - 1)
                picks.append((self.banks // 2 + q, self.short_row(owner)))
            lists.append(picks)
        return lists

    def own_picks(self, me):
        lists = []
        for s in range(self.far):
            to = me // 4 ^ s
            owner = self.near * to + me % 4
            q = self.far + jnp.minimum(to, self.short_far - 1)
            lists.append([(to, self.share * owner), (q, self.short_row(owner))])
        return lists

    def short_row(self, owner):
        owner = jnp.minimum(owner, self.long_blocks - 1)
        return jnp.where(
            owner < self.base_blocks,
            self.boxes + self.share * owner,
            self.half + self.share * (self.long_blocks - 1 - owner),
        )


def iota(shape, axis):
    return lax.broadcasted_iota(jnp.int32, shape, axis)


def long_image(cnt_ref):
    return jnp.where(cnt_ref[0, 1] > cnt_ref[0, 0], 1, 0)


def bank_kernel(plan, cols, firsts, carry, cnt_ref, pos_ref, boxes_hbm, bank_hbm, *rest):
    stat_ref = rest[0]
    chunks = len(firsts)
    outs = rest[1:1 + 2 * chunks]
    boxes_ref, x_v, bank_v, s_v, acc_v, box_sem, sems = rest[1 + 2 * chunks:]
    box_copy = pltpu.make_async_copy(boxes_hbm, boxes_ref, box_sem)
    box_copy.start()
    bank = bank_v.shape[0]
    tile = min(TILE, bank)

    def piece(i):
        rows = pl.ds(i * PIECE, PIECE)
        return pltpu.make_async_copy(bank_hbm.at[rows], bank_v.at[rows], sems.at[i])

    per = tile // PIECE
    for i in range(per):
        piece(i).start()
    box_copy.wait()
    half, base, boxes, flex = plan.half, plan.base, plan.boxes, plan.flex
    li = long_image(cnt_ref)
    si = 1 - li
    extra = cnt_ref[0, li] - half
    flip = (iota((flex, flex), 0) + iota((flex, flex), 1) == flex - 1).astype(BF16)
    back = jnp.dot(flip, boxes_ref[si, base:half, :], preferred_element_type=F32)
    front = boxes_ref[li, half:boxes, :].astype(F32)
    x_v[0:half, :] = boxes_ref[li, 0:half, :]
    x_v[half:boxes, :] = jnp.where(iota(front.shape, 0) < extra, front, back).astype(BF16)
    x_v[boxes:LIVE, :] = boxes_ref[si, 0:base, :]
    for i in range(per, min(2 * per, bank // PIECE)):
        piece(i).start()

    def scores(i, top):
        for k in range(per):
            piece(i * per + k).wait()

        @pl.when(i + 2 < bank // tile)
        def _():
            for k in range(per):
                piece((i + 2) * per + k).start()

        s = lax.dot_general(x_v[...], bank_v[pl.ds(i * tile, tile)], (((1,), (1,)), ((), ())),
                            preferred_element_type=F32)
        s_v[i] = s
        for j in range(tile // 128):
            top = jnp.maximum(top, s[:, j * 128:(j + 1) * 128])
        return top

    top = lax.fori_loop(0, bank // tile, scores, jnp.full((LIVE, 128), -jnp.inf, F32))
    peak = jnp.max(top, axis=1, keepdims=True)
    acc_v[...] = jnp.zeros_like(acc_v)

    def pulls(i, mass):
        e = jnp.exp(s_v[i] - peak)
        for j in range(tile // 128):
            mass = mass + e[:, j * 128:(j + 1) * 128]
        acc_v[...] += jnp.dot(e.astype(BF16), bank_v[pl.ds(i * tile, tile)],
                              preferred_element_type=F32)
        return mass

    mass = lax.fori_loop(0, bank // tile, pulls, jnp.zeros((LIVE, 128), F32))
    mass = jnp.sum(mass, axis=1, keepdims=True)
    both = jnp.where(iota((LIVE, 128), 1) == 0, peak, mass)
    lanes = jnp.transpose(both)[0:8, :]
    pad = jnp.zeros((1, 2 * boxes - LIVE), F32)
    packed = jnp.concatenate([
        lanes[0:1, 0:boxes],
        jnp.concatenate([lanes[0:1, boxes:LIVE], pad], axis=1),
        lanes[1:2, 0:boxes],
        jnp.concatenate([lanes[1:2, boxes:LIVE], pad], axis=1),
        jnp.zeros((4, boxes), F32)], axis=0)
    stat_ref[...] = packed
    share = plan.share
    for c, bit in enumerate(firsts):
        mine = pos_ref[0] // (1 << bit) % 2
        if carry[c]:
            rows = plan.half_rows(bit)
            outs[2 * c + 1][rows:rows + 8, :] = packed
        for kind, value in ((0, mine), (1, 1 - mine)):
            for q, row in enumerate(plan.half_blocks(bit, value)):
                outs[2 * c + kind][q * share:(q + 1) * share, :] = acc_v[
                    pl.ds(pl.multiple_of(row, 8), share), c * cols:(c + 1) * cols]


def merge_stats(tiles):
    peak = functools.reduce(jnp.maximum, [t[0:2, :] for t in tiles])
    factors = [jnp.exp(t[0:2, :] - peak) for t in tiles]
    mass = functools.reduce(jnp.add, [t[2:4, :] * f for t, f in zip(tiles, factors)])
    return peak, factors, mass


def store_columns(plan, values, col_ref):
    width = plan.boxes
    fill = [jnp.zeros((1, width), F32)] * (8 - len(values))
    top = jnp.transpose(jnp.concatenate([v[0:1, :] for v in values] + fill, axis=0))
    low = jnp.transpose(jnp.concatenate([v[1:2, :] for v in values] + fill, axis=0))
    col_ref[0:width, :] = top
    col_ref[width:LIVE, :] = low[0:LIVE - width, :]


def merge_kernel(plan, picks, has_tile, pos_ref, own_ref, got_ref, mine_ref, theirs_ref, *rest):
    outs, col_v = rest[:-1], rest[-1]
    share = plan.share
    peak, factors, mass = merge_stats([mine_ref[...], theirs_ref[...]])
    store_columns(plan, factors, col_v)
    for out_ref, blocks in zip(outs, picks(pos_ref[0])):
        for at, (q, row) in enumerate(blocks):
            src = pl.ds(pl.multiple_of(q * share, 8), share)
            col = col_v[pl.ds(pl.multiple_of(row, 8), share), :]
            out_ref[at * share:(at + 1) * share, :] = (
                own_ref[src, :] * col[:, 0:1] + got_ref[src, :] * col[:, 1:2])
        if has_tile:
            end = len(blocks) * share
            out_ref[end:end + 8, :] = jnp.concatenate([peak, mass, peak, mass], axis=0)


def conf_kernel(plan, cnt_ref, keep_ref, *refs):
    out_ref = refs[-1]
    base, boxes = plan.base, plan.boxes
    li = long_image(cnt_ref)
    keep_l = (keep_ref[pl.ds(li, 1), :] == 1).astype(F32)
    keep_s = (keep_ref[pl.ds(1 - li, 1), :] == 1).astype(F32)
    turn = (iota((boxes, boxes), 0) + iota((boxes, boxes), 1) == LIVE - 1).astype(BF16)
    turned = jnp.dot(jnp.broadcast_to(keep_s, (8, boxes)).astype(BF16), turn,
                     preferred_element_type=F32)[0:1, :]
    lane = iota((1, boxes), 1)
    live = jnp.concatenate([jnp.where(lane < cnt_ref[0, li], keep_l, turned),
                            jnp.where(lane < base, keep_s, 0.0)], axis=0)
    _, _, mass = merge_stats([r[...] for r in refs[:-1]])
    row = jnp.where(live > 0.5, -jnp.log(jnp.where(live > 0.5, mass, 1.0)), 0.0)
    total, count = jnp.sum(row), jnp.sum(live)
    out_ref[...] = jnp.where(iota((8, 128), 0) == 0, total, count)


def prep_kernel(plan, cnt_ref, pos_ref, keep_ref, *refs):
    far, share = plan.far, plan.share
    col_ref, neg_ref, norm_ref, col_v = refs[far:]
    me = pos_ref[0]
    li = long_image(cnt_ref)
    si = 1 - li
    peak, factors, mass = merge_stats([r[...] for r in refs[:far]])
    lane = iota((plan.boxes, 128), 1)
    src = iota((plan.boxes, 128), 0)
    slot = share * me + lane
    is_base = me < plan.base_blocks
    long_pick = (src == slot).astype(F32)
    short_pick = (src == jnp.where(is_base, slot, LIVE - 1 - slot)).astype(F32)
    keep = (keep_ref[...] == 1).astype(F32)
    stack = jnp.concatenate([peak, jnp.log(jnp.where(mass > 0.0, mass, 1.0)), mass, keep], axis=0)
    pick = functools.partial(jnp.dot, preferred_element_type=F32, precision=lax.Precision.HIGHEST)
    long_vals = pick(stack, long_pick)
    short_vals = pick(stack, short_pick)
    short_vals = jnp.where(is_base, pltpu.roll(short_vals, 7, 0), short_vals)
    slot_row = share * me + iota((1, 128), 1)
    live_rows = []
    for image, vals in ((li, long_vals), (si, short_vals)):
        kept = jnp.where(image == 0, long_vals[6:7, :], long_vals[7:8, :])
        live = (kept > 0.5) & (slot_row < cnt_ref[0, image])
        live_rows.append(live.astype(F32))
        norm = jnp.where(live, vals[0:1, :] + vals[2:3, :], 0.0)
        norm_ref[pl.ds(image, 1), :] = norm[:, 0:share]
        neg_ref[pl.ds(image, 1), :] = -vals[2:3, :]
        neg_ref[pl.ds(2 + image, 1), :] = live.astype(F32)
    live_cols = jnp.transpose(jnp.concatenate(live_rows + [jnp.zeros((6, 128), F32)], axis=0))
    weights = [f / jnp.where(mass > 0.0, mass, 1.0) for f in factors]
    for part in range(0, far, 6):
        store_columns(plan, weights[part:part + 6], col_v.at[part // 6])
    place = iota((share, 128), 1)
    for which, row in ((0, share * me), (1, plan.short_row(me))):
        out = jnp.where(place == far, live_cols[0:share, which:which + 1], 0.0)
        for s in range(far):
            col = col_v[s // 6, pl.ds(pl.multiple_of(row, 8), share), :]
            out = jnp.where(place == s, col[:, s % 6:s % 6 + 1], out)
        col_ref[which * share:(which + 1) * share, :] = out


def final_kernel(plan, chunks, images, cnt_ref, pos_ref, col_ref, neg_ref, *refs):
    far, share = plan.far, plan.share
    confs = refs[:images]
    pulls = refs[images:images + far * chunks]
    out_ref, prob_ref = refs[images + far * chunks:]
    me = pos_ref[0]
    li = long_image(cnt_ref)
    conf = functools.reduce(jnp.add, [c[...] for c in confs])
    mean = conf[0:1, 0:1] / jnp.maximum(conf[1:2, 0:1], 1.0)
    prob = jnp.where(neg_ref[2:4, :] > 0.5, neg_ref[0:2, :] - mean, 0.0)
    prob_ref[...] = prob[:, 0:share]
    width = pulls[0].shape[1]
    turned = (me >= plan.base_blocks) & (me < plan.long_blocks)
    a, b = iota((share, share), 0), iota((share, share), 1)
    order = (b == jnp.where(turned, share - 1 - a, a)).astype(BF16)
    for which, image in ((0, li), (1, 1 - li)):
        at = which * share
        col = col_ref[at:at + share, :]
        live = col[:, far:far + 1] > 0.5
        for c in range(chunks):
            value = functools.reduce(
                jnp.add, [pulls[c * far + s][at:at + share, :] * col[:, s:s + 1] for s in range(far)])
            value = value.astype(BF16)
            if which == 1:
                value = jnp.dot(order, value, preferred_element_type=F32).astype(BF16)
            out_ref[image, :, c * width:(c + 1) * width] = jnp.where(live, value, jnp.zeros_like(value))


VM = pl.BlockSpec(memory_space=pltpu.VMEM)
SM = pl.BlockSpec(memory_space=pltpu.SMEM)
HBM = pl.BlockSpec(memory_space=pltpu.HBM)
MIB = 2**20
VMEM_MIB = 52
FIRST_BIT = (0, 1, 0)


def call(body, ins, outs, scratch, flops, moved, limit, out_specs=None):
    return pl.pallas_call(
        body,
        out_shape=[jax.ShapeDtypeStruct(shape, dtype) for shape, dtype in outs],
        in_specs=ins,
        out_specs=out_specs or [VM] * len(outs),
        scratch_shapes=scratch,
        compiler_params=pltpu.CompilerParams(vmem_limit_bytes=limit * MIB),
        cost_estimate=pl.CostEstimate(flops=flops, bytes_accessed=moved, transcendentals=0),
    )


def on_device(boxes, prototypes, counts, keep):
    images, slots, width = boxes.shape
    bank = prototypes.shape[0]
    banks = lax.axis_size("bank")
    groups = lax.axis_size("img")
    plan = Plan(slots, banks)
    near, far, share = plan.near, plan.far, plan.share
    pos = lax.axis_index("bank").reshape(1)
    cols = slots
    chunks = width // cols
    firsts = [FIRST_BIT[c % len(FIRST_BIT)] for c in range(chunks)]
    carry = [bit not in firsts[:c] for c, bit in enumerate(firsts)]
    shapes = [((8, slots), F32)]
    for c in range(chunks):
        rows = plan.half_rows(firsts[c])
        shapes += [((rows, cols), F32), ((rows + 8 * carry[c], cols), F32)]
    stat, *parts = call(
        functools.partial(bank_kernel, plan, cols, firsts, carry),
        [SM, SM, HBM, HBM],
        shapes,
        [pltpu.VMEM(boxes.shape, BF16), pltpu.VMEM((LIVE, width), BF16),
         pltpu.VMEM((bank, width), BF16), pltpu.VMEM((bank // TILE, LIVE, TILE), F32),
         pltpu.VMEM((LIVE, width), F32), pltpu.SemaphoreType.DMA,
         pltpu.SemaphoreType.DMA((bank // PIECE,))],
        4 * LIVE * bank * width, bank * width * 2, VMEM_MIB,
    )(counts, pos, boxes, prototypes)

    def swap(array, step):
        return lax.ppermute(array, "bank", [(i, i ^ step) for i in range(banks)])

    def merge(picks, number, rows, has_tile, *arrays):
        return call(
            functools.partial(merge_kernel, plan, picks, has_tile),
            [SM] + [VM] * 4, [((rows + 8 * has_tile, cols), F32)] * number,
            [pltpu.VMEM((LIVE, 8), F32)],
            number * rows * cols * 4, number * rows * cols * 16, 8,
        )(pos, *arrays)

    got = [swap(parts[2 * c + 1], 1 << firsts[c]) for c in range(chunks)]
    first_tile = {firsts[c]: got[c][plan.half_rows(firsts[c]):] for c in range(chunks) if carry[c]}
    quarters = plan.quarter_rows()
    second_tiles = {}
    second = []
    for c, bit in enumerate(firsts):
        own, send = merge(functools.partial(plan.quarter_picks, bit), 2, quarters, carry[c],
                          parts[2 * c], got[c], stat, first_tile[bit])
        second.append((own, swap(send, 2 >> bit)))
        if carry[c]:
            second_tiles[bit] = (own[quarters:], second[c][1][quarters:])
    pulls = []
    for c, bit in enumerate(firsts):
        own, seen = second[c]
        if c == chunks - 1 and c > 0:
            own, pulls[-1][0] = lax.optimization_barrier((own, pulls[-1][0]))
        outs = merge(plan.own_picks, far, 2 * share, c == 0, own, seen, *second_tiles[bit])
        pulls.append([outs[0]] + [swap(outs[s], near * s) for s in range(1, far)])
    tiles = [p[2 * share:] for p in pulls[0]]

    conf, = call(functools.partial(conf_kernel, plan), [SM, VM] + [VM] * far, [((8, 128), F32)], [],
                 slots * 8, slots * 64, 4)(counts, keep, *tiles)
    confs = [conf] + [lax.ppermute(conf, "img", [(i, i ^ s) for i in range(groups)])
                      for s in range(1, groups)]
    col, neg, log_norm = call(
        functools.partial(prep_kernel, plan), [SM, SM, VM] + [VM] * far,
        [((2 * share, 128), F32), ((8, 128), F32), ((images, share), F32)],
        [pltpu.VMEM(((far + 5) // 6, LIVE, 8), F32)],
        slots * 8, slots * 64, 4,
    )(counts, pos, keep, *tiles)
    targets, top_logprob = call(
        functools.partial(final_kernel, plan, chunks, groups),
        [SM, SM, VM, VM] + [VM] * (groups + far * chunks),
        [((images, share, width), BF16), ((images, share), F32)], [],
        far * share * width * 4, far * share * width * 8, 8,
    )(counts, pos, col, neg, *confs, *[p for group in pulls for p in group])
    return targets, top_logprob, log_norm


def solution(mesh):
    placed = (P("img", None, None), P("bank", None), P("img", None), P("img", None))
    return jax.shard_map(
        on_device,
        mesh=mesh,
        in_specs=placed,
        out_specs=(P("img", "bank", None), P("img", "bank"), P("img", "bank")),
        check_vma=False,
    )
```

```python
import functools

import jax
import jax.numpy as jnp
from jax import lax
from jax.experimental import pallas as pl
from jax.experimental.pallas import tpu as pltpu
from jax.sharding import PartitionSpec as P


LIVE = 320
F32 = jnp.float32
BF16 = jnp.bfloat16
TILE = 2048
PIECE = 512


class Plan:
    def __init__(self, boxes, banks):
        self.boxes, self.banks = boxes, banks
        self.share = boxes // banks
        self.half = LIVE // 2
        self.base = LIVE - boxes
        self.flex = boxes - self.half
        self.near = 4
        self.far = banks // self.near
        self.long_blocks = self.half // self.share
        self.base_blocks = self.base // self.share
        self.short_far = -(-self.long_blocks // self.near)
        self.short_half = [sum(self.half_owner(b, i, 0) < self.long_blocks for i in range(banks // 2))
                           for b in (0, 1)]

    def half_owner(self, bit, i, value):
        if bit == 0:
            return 2 * i + value
        return i // 2 * 4 + 2 * value + i % 2

    def half_index(self, bit, owner):
        return owner // 2 if bit == 0 else owner // 4 * 2 + owner % 2

    def half_rows(self, bit):
        return self.share * (self.banks // 2 + self.short_half[bit])

    def half_blocks(self, bit, value):
        own = [self.half_owner(bit, i, value) for i in range(self.banks // 2)]
        return [self.share * o for o in own] + [self.short_row(o) for o in own[:self.short_half[bit]]]

    def quarter_rows(self):
        return self.share * (self.far + self.short_far)

    def quarter_picks(self, bit, me):
        lists = []
        for low in (me % 4, me % 4 ^ (2 >> bit)):
            picks = []
            for h in range(self.far):
                owner = self.near * h + low
                picks.append((self.half_index(bit, owner), self.share * owner))
            for h in range(self.short_far):
                owner = self.near * h + low
                q = jnp.minimum(self.half_index(bit, owner), self.short_half[bit] - 1)
                picks.append((self.banks // 2 + q, self.short_row(owner)))
            lists.append(picks)
        return lists

    def own_picks(self, me):
        lists = []
        for s in range(self.far):
            to = me // 4 ^ s
            owner = self.near * to + me % 4
            q = self.far + jnp.minimum(to, self.short_far - 1)
            lists.append([(to, self.share * owner), (q, self.short_row(owner))])
        return lists

    def short_row(self, owner):
        owner = jnp.minimum(owner, self.long_blocks - 1)
        return jnp.where(
            owner < self.base_blocks,
            self.boxes + self.share * owner,
            self.half + self.share * (self.long_blocks - 1 - owner),
        )


def iota(shape, axis):
    return lax.broadcasted_iota(jnp.int32, shape, axis)


def long_image(cnt_ref):
    return jnp.where(cnt_ref[0, 1] > cnt_ref[0, 0], 1, 0)


def bank_kernel(plan, cols, firsts, carry, cnt_ref, pos_ref, boxes_hbm, bank_hbm, *rest):
    stat_ref = rest[0]
    chunks = len(firsts)
    outs = rest[1:1 + 2 * chunks]
    boxes_ref, x_v, bank_v, s_v, acc_v, box_sem, sems = rest[1 + 2 * chunks:]
    box_copy = pltpu.make_async_copy(boxes_hbm, boxes_ref, box_sem)
    box_copy.start()
    bank = bank_v.shape[0]
    tile = min(TILE, bank)

    def piece(i):
        rows = pl.ds(i * PIECE, PIECE)
        return pltpu.make_async_copy(bank_hbm.at[rows], bank_v.at[rows], sems.at[i])

    per = tile // PIECE
    for i in range(per):
        piece(i).start()
    box_copy.wait()
    half, base, boxes, flex = plan.half, plan.base, plan.boxes, plan.flex
    li = long_image(cnt_ref)
    si = 1 - li
    extra = cnt_ref[0, li] - half
    flip = (iota((flex, flex), 0) + iota((flex, flex), 1) == flex - 1).astype(BF16)
    back = jnp.dot(flip, boxes_ref[si, base:half, :], preferred_element_type=F32)
    front = boxes_ref[li, half:boxes, :].astype(F32)
    x_v[0:half, :] = boxes_ref[li, 0:half, :]
    x_v[half:boxes, :] = jnp.where(iota(front.shape, 0) < extra, front, back).astype(BF16)
    x_v[boxes:LIVE, :] = boxes_ref[si, 0:base, :]
    for i in range(per, min(2 * per, bank // PIECE)):
        piece(i).start()

    def scores(i, top):
        for k in range(per):
            piece(i * per + k).wait()

        @pl.when(i + 2 < bank // tile)
        def _():
            for k in range(per):
                piece((i + 2) * per + k).start()

        s = lax.dot_general(x_v[...], bank_v[pl.ds(i * tile, tile)], (((1,), (1,)), ((), ())),
                            preferred_element_type=F32)
        s_v[i] = s
        for j in range(tile // 128):
            top = jnp.maximum(top, s[:, j * 128:(j + 1) * 128])
        return top

    top = lax.fori_loop(0, bank // tile, scores, jnp.full((LIVE, 128), -jnp.inf, F32))
    peak = jnp.max(top, axis=1, keepdims=True)
    acc_v[...] = jnp.zeros_like(acc_v)

    def pulls(i, mass):
        e = jnp.exp(s_v[i] - peak)
        for j in range(tile // 128):
            mass = mass + e[:, j * 128:(j + 1) * 128]
        acc_v[...] += jnp.dot(e.astype(BF16), bank_v[pl.ds(i * tile, tile)],
                              preferred_element_type=F32)
        return mass

    mass = lax.fori_loop(0, bank // tile, pulls, jnp.zeros((LIVE, 128), F32))
    mass = jnp.sum(mass, axis=1, keepdims=True)
    both = jnp.where(iota((LIVE, 128), 1) == 0, peak, mass)
    lanes = jnp.transpose(both)[0:8, :]
    pad = jnp.zeros((1, 2 * boxes - LIVE), F32)
    packed = jnp.concatenate([
        lanes[0:1, 0:boxes],
        jnp.concatenate([lanes[0:1, boxes:LIVE], pad], axis=1),
        lanes[1:2, 0:boxes],
        jnp.concatenate([lanes[1:2, boxes:LIVE], pad], axis=1),
        jnp.zeros((4, boxes), F32)], axis=0)
    stat_ref[...] = packed
    share = plan.share
    for c, bit in enumerate(firsts):
        mine = pos_ref[0] // (1 << bit) % 2
        if carry[c]:
            rows = plan.half_rows(bit)
            outs[2 * c + 1][rows:rows + 8, :] = packed
        for kind, value in ((0, mine), (1, 1 - mine)):
            for q, row in enumerate(plan.half_blocks(bit, value)):
                outs[2 * c + kind][q * share:(q + 1) * share, :] = acc_v[
                    pl.ds(pl.multiple_of(row, 8), share), c * cols:(c + 1) * cols]


def merge_stats(tiles):
    peak = functools.reduce(jnp.maximum, [t[0:2, :] for t in tiles])
    factors = [jnp.exp(t[0:2, :] - peak) for t in tiles]
    mass = functools.reduce(jnp.add, [t[2:4, :] * f for t, f in zip(tiles, factors)])
    return peak, factors, mass


def store_columns(plan, values, col_ref):
    width = plan.boxes
    fill = [jnp.zeros((1, width), F32)] * (8 - len(values))
    top = jnp.transpose(jnp.concatenate([v[0:1, :] for v in values] + fill, axis=0))
    low = jnp.transpose(jnp.concatenate([v[1:2, :] for v in values] + fill, axis=0))
    col_ref[0:width, :] = top
    col_ref[width:LIVE, :] = low[0:LIVE - width, :]


def merge_kernel(plan, picks, has_tile, pos_ref, own_ref, got_ref, mine_ref, theirs_ref, *rest):
    outs, col_v = rest[:-1], rest[-1]
    share = plan.share
    peak, factors, mass = merge_stats([mine_ref[...], theirs_ref[...]])
    store_columns(plan, factors, col_v)
    for out_ref, blocks in zip(outs, picks(pos_ref[0])):
        for at, (q, row) in enumerate(blocks):
            src = pl.ds(pl.multiple_of(q * share, 8), share)
            col = col_v[pl.ds(pl.multiple_of(row, 8), share), :]
            out_ref[at * share:(at + 1) * share, :] = (
                own_ref[src, :] * col[:, 0:1] + got_ref[src, :] * col[:, 1:2])
        if has_tile:
            end = len(blocks) * share
            out_ref[end:end + 8, :] = jnp.concatenate([peak, mass, peak, mass], axis=0)


def live_kernel(plan, cnt_ref, keep_ref, live_ref):
    base, boxes = plan.base, plan.boxes
    li = long_image(cnt_ref)
    keep_l = (keep_ref[pl.ds(li, 1), :] == 1).astype(F32)
    keep_s = (keep_ref[pl.ds(1 - li, 1), :] == 1).astype(F32)
    turn = (iota((boxes, boxes), 0) + iota((boxes, boxes), 1) == LIVE - 1).astype(BF16)
    turned = jnp.dot(jnp.broadcast_to(keep_s, (8, boxes)).astype(BF16), turn,
                     preferred_element_type=F32)[0:1, :]
    lane = iota((1, boxes), 1)
    live_ref[0:1, :] = jnp.where(lane < cnt_ref[0, li], keep_l, turned)
    live_ref[1:2, :] = jnp.where(lane < base, keep_s, 0.0)
    live_ref[2:8, :] = jnp.zeros((6, boxes), F32)


def conf_kernel(live_ref, *refs):
    out_ref = refs[-1]
    _, _, mass = merge_stats([r[...] for r in refs[:-1]])
    live = live_ref[0:2, :]
    row = jnp.where(live > 0.5, -jnp.log(jnp.where(live > 0.5, mass, 1.0)), 0.0)
    total, count = jnp.sum(row), jnp.sum(live)
    out_ref[...] = jnp.where(iota((8, 128), 0) == 0, total, count)


def prep_kernel(plan, cnt_ref, pos_ref, keep_ref, *refs):
    far, share = plan.far, plan.share
    col_ref, neg_ref, norm_ref, col_v = refs[far:]
    me = pos_ref[0]
    li = long_image(cnt_ref)
    si = 1 - li
    peak, factors, mass = merge_stats([r[...] for r in refs[:far]])
    lane = iota((plan.boxes, 128), 1)
    src = iota((plan.boxes, 128), 0)
    slot = share * me + lane
    is_base = me < plan.base_blocks
    long_pick = (src == slot).astype(F32)
    short_pick = (src == jnp.where(is_base, slot, LIVE - 1 - slot)).astype(F32)
    keep = (keep_ref[...] == 1).astype(F32)
    stack = jnp.concatenate([peak, jnp.log(jnp.where(mass > 0.0, mass, 1.0)), mass, keep], axis=0)
    pick = functools.partial(jnp.dot, preferred_element_type=F32, precision=lax.Precision.HIGHEST)
    long_vals = pick(stack, long_pick)
    short_vals = pick(stack, short_pick)
    short_vals = jnp.where(is_base, pltpu.roll(short_vals, 7, 0), short_vals)
    slot_row = share * me + iota((1, 128), 1)
    live_rows = []
    for image, vals in ((li, long_vals), (si, short_vals)):
        kept = jnp.where(image == 0, long_vals[6:7, :], long_vals[7:8, :])
        live = (kept > 0.5) & (slot_row < cnt_ref[0, image])
        live_rows.append(live.astype(F32))
        norm = jnp.where(live, vals[0:1, :] + vals[2:3, :], 0.0)
        norm_ref[pl.ds(image, 1), :] = norm[:, 0:share]
        neg_ref[pl.ds(image, 1), :] = -vals[2:3, :]
        neg_ref[pl.ds(2 + image, 1), :] = live.astype(F32)
    live_cols = jnp.transpose(jnp.concatenate(live_rows + [jnp.zeros((6, 128), F32)], axis=0))
    weights = [f / jnp.where(mass > 0.0, mass, 1.0) for f in factors]
    for part in range(0, far, 6):
        store_columns(plan, weights[part:part + 6], col_v.at[part // 6])
    place = iota((share, 128), 1)
    for which, row in ((0, share * me), (1, plan.short_row(me))):
        out = jnp.where(place == far, live_cols[0:share, which:which + 1], 0.0)
        for s in range(far):
            col = col_v[s // 6, pl.ds(pl.multiple_of(row, 8), share), :]
            out = jnp.where(place == s, col[:, s % 6:s % 6 + 1], out)
        col_ref[which * share:(which + 1) * share, :] = out


def final_kernel(plan, chunks, images, cnt_ref, pos_ref, col_ref, neg_ref, *refs):
    far, share = plan.far, plan.share
    confs = refs[:images]
    pulls = refs[images:images + far * chunks]
    out_ref, prob_ref = refs[images + far * chunks:]
    me = pos_ref[0]
    li = long_image(cnt_ref)
    conf = functools.reduce(jnp.add, [c[...] for c in confs])
    mean = conf[0:1, 0:1] / jnp.maximum(conf[1:2, 0:1], 1.0)
    prob = jnp.where(neg_ref[2:4, :] > 0.5, neg_ref[0:2, :] - mean, 0.0)
    prob_ref[...] = prob[:, 0:share]
    width = pulls[0].shape[1]
    turned = (me >= plan.base_blocks) & (me < plan.long_blocks)
    a, b = iota((share, share), 0), iota((share, share), 1)
    order = (b == jnp.where(turned, share - 1 - a, a)).astype(BF16)
    for which, image in ((0, li), (1, 1 - li)):
        at = which * share
        col = col_ref[at:at + share, :]
        live = col[:, far:far + 1] > 0.5
        for c in range(chunks):
            value = functools.reduce(
                jnp.add, [pulls[c * far + s][at:at + share, :] * col[:, s:s + 1] for s in range(far)])
            value = value.astype(BF16)
            if which == 1:
                value = jnp.dot(order, value, preferred_element_type=F32).astype(BF16)
            out_ref[image, :, c * width:(c + 1) * width] = jnp.where(live, value, jnp.zeros_like(value))


VM = pl.BlockSpec(memory_space=pltpu.VMEM)
SM = pl.BlockSpec(memory_space=pltpu.SMEM)
HBM = pl.BlockSpec(memory_space=pltpu.HBM)
MIB = 2**20
VMEM_MIB = 52
FIRST_BIT = (0, 1, 0)


def call(body, ins, outs, scratch, flops, moved, limit, out_specs=None):
    return pl.pallas_call(
        body,
        out_shape=[jax.ShapeDtypeStruct(shape, dtype) for shape, dtype in outs],
        in_specs=ins,
        out_specs=out_specs or [VM] * len(outs),
        scratch_shapes=scratch,
        compiler_params=pltpu.CompilerParams(vmem_limit_bytes=limit * MIB),
        cost_estimate=pl.CostEstimate(flops=flops, bytes_accessed=moved, transcendentals=0),
    )


def on_device(boxes, prototypes, counts, keep):
    images, slots, width = boxes.shape
    bank = prototypes.shape[0]
    banks = lax.axis_size("bank")
    groups = lax.axis_size("img")
    plan = Plan(slots, banks)
    near, far, share = plan.near, plan.far, plan.share
    pos = lax.axis_index("bank").reshape(1)
    cols = slots
    chunks = width // cols
    firsts = [FIRST_BIT[c % len(FIRST_BIT)] for c in range(chunks)]
    carry = [bit not in firsts[:c] for c, bit in enumerate(firsts)]
    shapes = [((8, slots), F32)]
    for c in range(chunks):
        rows = plan.half_rows(firsts[c])
        shapes += [((rows, cols), F32), ((rows + 8 * carry[c], cols), F32)]
    stat, *parts = call(
        functools.partial(bank_kernel, plan, cols, firsts, carry),
        [SM, SM, HBM, HBM],
        shapes,
        [pltpu.VMEM(boxes.shape, BF16), pltpu.VMEM((LIVE, width), BF16),
         pltpu.VMEM((bank, width), BF16), pltpu.VMEM((bank // TILE, LIVE, TILE), F32),
         pltpu.VMEM((LIVE, width), F32), pltpu.SemaphoreType.DMA,
         pltpu.SemaphoreType.DMA((bank // PIECE,))],
        4 * LIVE * bank * width, bank * width * 2, VMEM_MIB,
    )(counts, pos, boxes, prototypes)

    def swap(array, step):
        return lax.ppermute(array, "bank", [(i, i ^ step) for i in range(banks)])

    def merge(picks, number, rows, has_tile, *arrays):
        return call(
            functools.partial(merge_kernel, plan, picks, has_tile),
            [SM] + [VM] * 4, [((rows + 8 * has_tile, cols), F32)] * number,
            [pltpu.VMEM((LIVE, 8), F32)],
            number * rows * cols * 4, number * rows * cols * 16, 8,
        )(pos, *arrays)

    live, = call(functools.partial(live_kernel, plan), [SM, VM], [((8, slots), F32)], [],
                 slots * 8, slots * 64, 4)(counts, keep)
    got = [swap(parts[2 * c + 1], 1 << firsts[c]) for c in range(chunks)]
    first_tile = {firsts[c]: got[c][plan.half_rows(firsts[c]):] for c in range(chunks) if carry[c]}
    quarters = plan.quarter_rows()
    second_tiles = {}
    second = []
    for c, bit in enumerate(firsts):
        own, send = merge(functools.partial(plan.quarter_picks, bit), 2, quarters, carry[c],
                          parts[2 * c], got[c], stat, first_tile[bit])
        second.append((own, swap(send, 2 >> bit)))
        if carry[c]:
            second_tiles[bit] = (own[quarters:], second[c][1][quarters:])
    pulls = []
    for c, bit in enumerate(firsts):
        own, seen = second[c]
        if c == 0:
            own, live = lax.optimization_barrier((own, live))
        if c == chunks - 1 and c > 0:
            own, pulls[-1][0] = lax.optimization_barrier((own, pulls[-1][0]))
        outs = merge(plan.own_picks, far, 2 * share, c == 0, own, seen, *second_tiles[bit])
        pulls.append([outs[0]] + [swap(outs[s], near * s) for s in range(1, far)])
    tiles = [p[2 * share:] for p in pulls[0]]

    conf, = call(conf_kernel, [VM] * (1 + far), [((8, 128), F32)], [],
                 slots * 8, slots * 64, 4)(live, *tiles)
    confs = [conf] + [lax.ppermute(conf, "img", [(i, i ^ s) for i in range(groups)])
                      for s in range(1, groups)]
    col, neg, log_norm = call(
        functools.partial(prep_kernel, plan), [SM, SM, VM] + [VM] * far,
        [((2 * share, 128), F32), ((8, 128), F32), ((images, share), F32)],
        [pltpu.VMEM(((far + 5) // 6, LIVE, 8), F32)],
        slots * 8, slots * 64, 4,
    )(counts, pos, keep, *tiles)
    targets, top_logprob = call(
        functools.partial(final_kernel, plan, chunks, groups),
        [SM, SM, VM, VM] + [VM] * (groups + far * chunks),
        [((images, share, width), BF16), ((images, share), F32)], [],
        far * share * width * 4, far * share * width * 8, 8,
    )(counts, pos, col, neg, *confs, *[p for group in pulls for p in group])
    return targets, top_logprob, log_norm


def solution(mesh):
    placed = (P("img", None, None), P("bank", None), P("img", None), P("img", None))
    return jax.shard_map(
        on_device,
        mesh=mesh,
        in_specs=placed,
        out_specs=(P("img", "bank", None), P("img", "bank"), P("img", "bank")),
        check_vma=False,
    )
```

```python
import functools

import jax
import jax.numpy as jnp
from jax import lax
from jax.experimental import pallas as pl
from jax.experimental.pallas import tpu as pltpu
from jax.sharding import PartitionSpec as P


LIVE = 320
F32 = jnp.float32
BF16 = jnp.bfloat16
TILE = 2048
PIECE = 512


class Plan:
    def __init__(self, boxes, banks):
        self.boxes, self.banks = boxes, banks
        self.share = boxes // banks
        self.half = LIVE // 2
        self.base = LIVE - boxes
        self.flex = boxes - self.half
        self.near = 4
        self.far = banks // self.near
        self.long_blocks = self.half // self.share
        self.base_blocks = self.base // self.share
        self.short_far = -(-self.long_blocks // self.near)
        self.short_half = [sum(self.half_owner(b, i, 0) < self.long_blocks for i in range(banks // 2))
                           for b in (0, 1)]

    def half_owner(self, bit, i, value):
        if bit == 0:
            return 2 * i + value
        return i // 2 * 4 + 2 * value + i % 2

    def half_index(self, bit, owner):
        return owner // 2 if bit == 0 else owner // 4 * 2 + owner % 2

    def half_rows(self, bit):
        return self.share * (self.banks // 2 + self.short_half[bit])

    def half_blocks(self, bit, value):
        own = [self.half_owner(bit, i, value) for i in range(self.banks // 2)]
        return [self.share * o for o in own] + [self.short_row(o) for o in own[:self.short_half[bit]]]

    def quarter_rows(self):
        return self.share * (self.far + self.short_far)

    def quarter_picks(self, bit, me):
        lists = []
        for low in (me % 4, me % 4 ^ (2 >> bit)):
            picks = []
            for h in range(self.far):
                owner = self.near * h + low
                picks.append((self.half_index(bit, owner), self.share * owner))
            for h in range(self.short_far):
                owner = self.near * h + low
                q = jnp.minimum(self.half_index(bit, owner), self.short_half[bit] - 1)
                picks.append((self.banks // 2 + q, self.short_row(owner)))
            lists.append(picks)
        return lists

    def own_picks(self, me):
        lists = []
        for s in range(self.far):
            to = me // 4 ^ s
            owner = self.near * to + me % 4
            q = self.far + jnp.minimum(to, self.short_far - 1)
            lists.append([(to, self.share * owner), (q, self.short_row(owner))])
        return lists

    def short_row(self, owner):
        owner = jnp.minimum(owner, self.long_blocks - 1)
        return jnp.where(
            owner < self.base_blocks,
            self.boxes + self.share * owner,
            self.half + self.share * (self.long_blocks - 1 - owner),
        )


def iota(shape, axis):
    return lax.broadcasted_iota(jnp.int32, shape, axis)


def long_image(cnt_ref):
    return jnp.where(cnt_ref[0, 1] > cnt_ref[0, 0], 1, 0)


def bank_kernel(plan, cols, firsts, carry, cnt_ref, pos_ref, boxes_hbm, bank_hbm, *rest):
    stat_ref = rest[0]
    chunks = len(firsts)
    outs = rest[1:1 + 2 * chunks]
    boxes_ref, x_v, bank_v, s_v, acc_v, box_sem, sems = rest[1 + 2 * chunks:]
    box_copy = pltpu.make_async_copy(boxes_hbm, boxes_ref, box_sem)
    box_copy.start()
    bank = bank_v.shape[0]
    tile = min(TILE, bank)

    def piece(i):
        rows = pl.ds(i * PIECE, PIECE)
        return pltpu.make_async_copy(bank_hbm.at[rows], bank_v.at[rows], sems.at[i])

    per = tile // PIECE
    for i in range(per):
        piece(i).start()
    box_copy.wait()
    half, base, boxes, flex = plan.half, plan.base, plan.boxes, plan.flex
    li = long_image(cnt_ref)
    si = 1 - li
    extra = cnt_ref[0, li] - half
    flip = (iota((flex, flex), 0) + iota((flex, flex), 1) == flex - 1).astype(BF16)
    back = jnp.dot(flip, boxes_ref[si, base:half, :], preferred_element_type=F32)
    front = boxes_ref[li, half:boxes, :].astype(F32)
    x_v[0:half, :] = boxes_ref[li, 0:half, :]
    x_v[half:boxes, :] = jnp.where(iota(front.shape, 0) < extra, front, back).astype(BF16)
    x_v[boxes:LIVE, :] = boxes_ref[si, 0:base, :]
    for i in range(per, min(2 * per, bank // PIECE)):
        piece(i).start()

    def scores(i, top):
        for k in range(per):
            piece(i * per + k).wait()

        @pl.when(i + 2 < bank // tile)
        def _():
            for k in range(per):
                piece((i + 2) * per + k).start()

        s = lax.dot_general(x_v[...], bank_v[pl.ds(i * tile, tile)], (((1,), (1,)), ((), ())),
                            preferred_element_type=F32)
        s_v[i] = s
        for j in range(tile // 128):
            top = jnp.maximum(top, s[:, j * 128:(j + 1) * 128])
        return top

    top = lax.fori_loop(0, bank // tile, scores, jnp.full((LIVE, 128), -jnp.inf, F32))
    peak = jnp.max(top, axis=1, keepdims=True)
    acc_v[...] = jnp.zeros_like(acc_v)

    def pulls(i, mass):
        e = jnp.exp(s_v[i] - peak)
        for j in range(tile // 128):
            mass = mass + e[:, j * 128:(j + 1) * 128]
        acc_v[...] += jnp.dot(e.astype(BF16), bank_v[pl.ds(i * tile, tile)],
                              preferred_element_type=F32)
        return mass

    mass = lax.fori_loop(0, bank // tile, pulls, jnp.zeros((LIVE, 128), F32))
    mass = jnp.sum(mass, axis=1, keepdims=True)
    both = jnp.where(iota((LIVE, 128), 1) == 0, peak, mass)
    lanes = jnp.transpose(both)[0:8, :]
    pad = jnp.zeros((1, 2 * boxes - LIVE), F32)
    packed = jnp.concatenate([
        lanes[0:1, 0:boxes],
        jnp.concatenate([lanes[0:1, boxes:LIVE], pad], axis=1),
        lanes[1:2, 0:boxes],
        jnp.concatenate([lanes[1:2, boxes:LIVE], pad], axis=1),
        jnp.zeros((4, boxes), F32)], axis=0)
    stat_ref[...] = packed
    share = plan.share
    for c, bit in enumerate(firsts):
        mine = pos_ref[0] // (1 << bit) % 2
        if carry[c]:
            rows = plan.half_rows(bit)
            outs[2 * c + 1][rows:rows + 8, :] = packed
        for kind, value in ((0, mine), (1, 1 - mine)):
            for q, row in enumerate(plan.half_blocks(bit, value)):
                outs[2 * c + kind][q * share:(q + 1) * share, :] = acc_v[
                    pl.ds(pl.multiple_of(row, 8), share), c * cols:(c + 1) * cols]


def merge_stats(tiles):
    peak = functools.reduce(jnp.maximum, [t[0:2, :] for t in tiles])
    factors = [jnp.exp(t[0:2, :] - peak) for t in tiles]
    mass = functools.reduce(jnp.add, [t[2:4, :] * f for t, f in zip(tiles, factors)])
    return peak, factors, mass


def store_columns(plan, values, col_ref):
    width = plan.boxes
    fill = [jnp.zeros((1, width), F32)] * (8 - len(values))
    top = jnp.transpose(jnp.concatenate([v[0:1, :] for v in values] + fill, axis=0))
    low = jnp.transpose(jnp.concatenate([v[1:2, :] for v in values] + fill, axis=0))
    col_ref[0:width, :] = top
    col_ref[width:LIVE, :] = low[0:LIVE - width, :]


def merge_kernel(plan, picks, has_tile, pos_ref, own_ref, got_ref, mine_ref, theirs_ref, *rest):
    outs, col_v = rest[:-1], rest[-1]
    share = plan.share
    peak, factors, mass = merge_stats([mine_ref[...], theirs_ref[...]])
    store_columns(plan, factors, col_v)
    for out_ref, blocks in zip(outs, picks(pos_ref[0])):
        for at, (q, row) in enumerate(blocks):
            src = pl.ds(pl.multiple_of(q * share, 8), share)
            col = col_v[pl.ds(pl.multiple_of(row, 8), share), :]
            out_ref[at * share:(at + 1) * share, :] = (
                own_ref[src, :] * col[:, 0:1] + got_ref[src, :] * col[:, 1:2])
        if has_tile:
            end = len(blocks) * share
            out_ref[end:end + 8, :] = jnp.concatenate([peak, mass, peak, mass], axis=0)


def live_kernel(plan, cnt_ref, keep_ref, live_ref):
    base, boxes = plan.base, plan.boxes
    li = long_image(cnt_ref)
    keep_l = (keep_ref[pl.ds(li, 1), :] == 1).astype(F32)
    keep_s = (keep_ref[pl.ds(1 - li, 1), :] == 1).astype(F32)
    turn = (iota((boxes, boxes), 0) + iota((boxes, boxes), 1) == LIVE - 1).astype(BF16)
    turned = jnp.dot(jnp.broadcast_to(keep_s, (8, boxes)).astype(BF16), turn,
                     preferred_element_type=F32)[0:1, :]
    lane = iota((1, boxes), 1)
    live_ref[0:1, :] = jnp.where(lane < cnt_ref[0, li], keep_l, turned)
    live_ref[1:2, :] = jnp.where(lane < base, keep_s, 0.0)
    live_ref[2:8, :] = jnp.zeros((6, boxes), F32)


def conf_kernel(live_ref, *refs):
    out_ref = refs[-1]
    _, _, mass = merge_stats([r[...] for r in refs[:-1]])
    live = live_ref[0:2, :]
    row = jnp.where(live > 0.5, -jnp.log(jnp.where(live > 0.5, mass, 1.0)), 0.0)
    total, count = jnp.sum(row), jnp.sum(live)
    out_ref[...] = jnp.where(iota((8, 128), 0) == 0, total, count)


def prep_kernel(plan, cnt_ref, pos_ref, keep_ref, *refs):
    far, share = plan.far, plan.share
    col_ref, neg_ref, norm_ref, col_v = refs[far:]
    me = pos_ref[0]
    li = long_image(cnt_ref)
    si = 1 - li
    peak, factors, mass = merge_stats([r[...] for r in refs[:far]])
    lane = iota((plan.boxes, 128), 1)
    src = iota((plan.boxes, 128), 0)
    slot = share * me + lane
    is_base = me < plan.base_blocks
    long_pick = (src == slot).astype(F32)
    short_pick = (src == jnp.where(is_base, slot, LIVE - 1 - slot)).astype(F32)
    keep = (keep_ref[...] == 1).astype(F32)
    stack = jnp.concatenate([peak, jnp.log(jnp.where(mass > 0.0, mass, 1.0)), mass, keep], axis=0)
    pick = functools.partial(jnp.dot, preferred_element_type=F32, precision=lax.Precision.HIGHEST)
    long_vals = pick(stack, long_pick)
    short_vals = pick(stack, short_pick)
    short_vals = jnp.where(is_base, pltpu.roll(short_vals, 7, 0), short_vals)
    slot_row = share * me + iota((1, 128), 1)
    live_rows = []
    for image, vals in ((li, long_vals), (si, short_vals)):
        kept = jnp.where(image == 0, long_vals[6:7, :], long_vals[7:8, :])
        live = (kept > 0.5) & (slot_row < cnt_ref[0, image])
        live_rows.append(live.astype(F32))
        norm = jnp.where(live, vals[0:1, :] + vals[2:3, :], 0.0)
        norm_ref[pl.ds(image, 1), :] = norm[:, 0:share]
        neg_ref[pl.ds(image, 1), :] = -vals[2:3, :]
        neg_ref[pl.ds(2 + image, 1), :] = live.astype(F32)
    live_cols = jnp.transpose(jnp.concatenate(live_rows + [jnp.zeros((6, 128), F32)], axis=0))
    weights = [f / jnp.where(mass > 0.0, mass, 1.0) for f in factors]
    for part in range(0, far, 6):
        store_columns(plan, weights[part:part + 6], col_v.at[part // 6])
    place = iota((share, 128), 1)
    for which, row in ((0, share * me), (1, plan.short_row(me))):
        out = jnp.where(place == far, live_cols[0:share, which:which + 1], 0.0)
        for s in range(far):
            col = col_v[s // 6, pl.ds(pl.multiple_of(row, 8), share), :]
            out = jnp.where(place == s, col[:, s % 6:s % 6 + 1], out)
        col_ref[which * share:(which + 1) * share, :] = out


def final_kernel(plan, chunks, images, cnt_ref, pos_ref, col_ref, neg_ref, *refs):
    far, share = plan.far, plan.share
    confs = refs[:images]
    pulls = refs[images:images + far * chunks]
    out_ref, prob_ref = refs[images + far * chunks:]
    me = pos_ref[0]
    li = long_image(cnt_ref)
    conf = functools.reduce(jnp.add, [c[...] for c in confs])
    mean = conf[0:1, 0:1] / jnp.maximum(conf[1:2, 0:1], 1.0)
    prob = jnp.where(neg_ref[2:4, :] > 0.5, neg_ref[0:2, :] - mean, 0.0)
    prob_ref[...] = prob[:, 0:share]
    width = pulls[0].shape[1]
    turned = (me >= plan.base_blocks) & (me < plan.long_blocks)
    a, b = iota((share, share), 0), iota((share, share), 1)
    order = (b == jnp.where(turned, share - 1 - a, a)).astype(BF16)
    for which, image in ((0, li), (1, 1 - li)):
        at = which * share
        col = col_ref[at:at + share, :]
        live = col[:, far:far + 1] > 0.5
        for c in range(chunks):
            value = functools.reduce(
                jnp.add, [pulls[c * far + s][at:at + share, :] * col[:, s:s + 1] for s in range(far)])
            value = value.astype(BF16)
            if which == 1:
                value = jnp.dot(order, value, preferred_element_type=F32).astype(BF16)
            out_ref[image, :, c * width:(c + 1) * width] = jnp.where(live, value, jnp.zeros_like(value))


VM = pl.BlockSpec(memory_space=pltpu.VMEM)
SM = pl.BlockSpec(memory_space=pltpu.SMEM)
HBM = pl.BlockSpec(memory_space=pltpu.HBM)
MIB = 2**20
VMEM_MIB = 52
FIRST_BIT = (0, 0, 1)


def call(body, ins, outs, scratch, flops, moved, limit, out_specs=None):
    return pl.pallas_call(
        body,
        out_shape=[jax.ShapeDtypeStruct(shape, dtype) for shape, dtype in outs],
        in_specs=ins,
        out_specs=out_specs or [VM] * len(outs),
        scratch_shapes=scratch,
        compiler_params=pltpu.CompilerParams(vmem_limit_bytes=limit * MIB),
        cost_estimate=pl.CostEstimate(flops=flops, bytes_accessed=moved, transcendentals=0),
    )


def on_device(boxes, prototypes, counts, keep):
    images, slots, width = boxes.shape
    bank = prototypes.shape[0]
    banks = lax.axis_size("bank")
    groups = lax.axis_size("img")
    plan = Plan(slots, banks)
    near, far, share = plan.near, plan.far, plan.share
    pos = lax.axis_index("bank").reshape(1)
    cols = slots
    chunks = width // cols
    firsts = [FIRST_BIT[c % len(FIRST_BIT)] for c in range(chunks)]
    carry = [bit not in firsts[:c] for c, bit in enumerate(firsts)]
    shapes = [((8, slots), F32)]
    for c in range(chunks):
        rows = plan.half_rows(firsts[c])
        shapes += [((rows, cols), F32), ((rows + 8 * carry[c], cols), F32)]
    stat, *parts = call(
        functools.partial(bank_kernel, plan, cols, firsts, carry),
        [SM, SM, HBM, HBM],
        shapes,
        [pltpu.VMEM(boxes.shape, BF16), pltpu.VMEM((LIVE, width), BF16),
         pltpu.VMEM((bank, width), BF16), pltpu.VMEM((bank // TILE, LIVE, TILE), F32),
         pltpu.VMEM((LIVE, width), F32), pltpu.SemaphoreType.DMA,
         pltpu.SemaphoreType.DMA((bank // PIECE,))],
        4 * LIVE * bank * width, bank * width * 2, VMEM_MIB,
    )(counts, pos, boxes, prototypes)

    def swap(array, step):
        return lax.ppermute(array, "bank", [(i, i ^ step) for i in range(banks)])

    def merge(picks, number, rows, has_tile, *arrays):
        return call(
            functools.partial(merge_kernel, plan, picks, has_tile),
            [SM] + [VM] * 4, [((rows + 8 * has_tile, cols), F32)] * number,
            [pltpu.VMEM((LIVE, 8), F32)],
            number * rows * cols * 4, number * rows * cols * 16, 8,
        )(pos, *arrays)

    live, = call(functools.partial(live_kernel, plan), [SM, VM], [((8, slots), F32)], [],
                 slots * 8, slots * 64, 4)(counts, keep)
    got = [swap(parts[2 * c + 1], 1 << firsts[c]) for c in range(chunks)]
    got[0], live = lax.optimization_barrier((got[0], live))
    first_tile = {firsts[c]: got[c][plan.half_rows(firsts[c]):] for c in range(chunks) if carry[c]}
    quarters = plan.quarter_rows()
    second_tiles = {}
    second = []
    for c, bit in enumerate(firsts):
        own, send = merge(functools.partial(plan.quarter_picks, bit), 2, quarters, carry[c],
                          parts[2 * c], got[c], stat, first_tile[bit])
        second.append((own, swap(send, 2 >> bit)))
        if carry[c]:
            second_tiles[bit] = (own[quarters:], second[c][1][quarters:])
    pulls = []
    for c, bit in enumerate(firsts):
        own, seen = second[c]
        if c == chunks - 1 and c > 0:
            own, pulls[-1][0] = lax.optimization_barrier((own, pulls[-1][0]))
        outs = merge(plan.own_picks, far, 2 * share, c == 0, own, seen, *second_tiles[bit])
        pulls.append([outs[0]] + [swap(outs[s], near * s) for s in range(1, far)])
    tiles = [p[2 * share:] for p in pulls[0]]

    conf, = call(conf_kernel, [VM] * (1 + far), [((8, 128), F32)], [],
                 slots * 8, slots * 64, 4)(live, *tiles)
    confs = [conf] + [lax.ppermute(conf, "img", [(i, i ^ s) for i in range(groups)])
                      for s in range(1, groups)]
    col, neg, log_norm = call(
        functools.partial(prep_kernel, plan), [SM, SM, VM] + [VM] * far,
        [((2 * share, 128), F32), ((8, 128), F32), ((images, share), F32)],
        [pltpu.VMEM(((far + 5) // 6, LIVE, 8), F32)],
        slots * 8, slots * 64, 4,
    )(counts, pos, keep, *tiles)
    targets, top_logprob = call(
        functools.partial(final_kernel, plan, chunks, groups),
        [SM, SM, VM, VM] + [VM] * (groups + far * chunks),
        [((images, share, width), BF16), ((images, share), F32)], [],
        far * share * width * 4, far * share * width * 8, 8,
    )(counts, pos, col, neg, *confs, *[p for group in pulls for p in group])
    return targets, top_logprob, log_norm


def solution(mesh):
    placed = (P("img", None, None), P("bank", None), P("img", None), P("img", None))
    return jax.shard_map(
        on_device,
        mesh=mesh,
        in_specs=placed,
        out_specs=(P("img", "bank", None), P("img", "bank"), P("img", "bank")),
        check_vma=False,
    )
```
